32 devices in a mesh: grid: 8 (over y, x, core), mode: 4 (over z).
Axes of the slice: x: 2, y: 2, z: 4, core: 2. Of those that a mesh axis runs over, the one named last changes fastest.
Arguments:
- held_modes: bfloat16 [224, 3, 32, 4, 128], P('mode', None, 'grid'), may hold values from -6 to 6
- new_modes: bfloat16 [32, 3, 32, 4, 128], P('mode', None, 'grid'), may hold values from -6 to 6
Outputs:
- new_third: float32 [256, 8192], P('grid', 'mode')
- held_third_new_first: float32 [256, 7168], P('grid', 'mode')
- held_third_new_second: float32 [224, 7168], P('grid', 'mode')
The draws below stay inside these ranges and needn't reach their ends.
All inputs are finite; a program needn't handle non-finite values.
Results may differ from the reference program's by a relative error of at most 0.0042.
Values may be sent and summed in bfloat16 or wider, within the bound.
No kernel may reach another device: no remote copies, remote signals or barrier semaphores. Data moves between devices by JAX's collectives and lax.ppermute only.
A program may use at most 128 MiB of HBM per device.

```python
import math
import jax
import jax.numpy as jnp
from jax import lax

HELD = 224
NEW = 32
MODES = 256
NY = 4
NZ = 128
NX = 32


def steps_of(key, extent, split, low, largest):
    gain, own = 1.0, jax.random.fold_in(key, 6)
    for axis_at, parts in split:
        draws = jnp.exp(jax.random.uniform(jax.random.fold_in(own, axis_at), (parts,), jnp.float32, low / len(split), largest / len(split)))
        gain = gain * jnp.repeat(draws, extent[axis_at] // parts).reshape([-1 if axis == axis_at else 1 for axis in range(len(extent))])
    return gain


def noise(rng, extent, spread, bound, pieces=(), dtype=jnp.bfloat16):
    result = jax.random.normal(rng, extent, jnp.float32) * spread
    if len(pieces) > 0:
        result = steps_of(rng, extent, pieces, -0.22, 0.18) * result
    return jnp.clip(result, min=-bound, max=bound).astype(dtype)


def setup_inputs(seed: int = 0) -> dict:
    splits = jax.random.split(jax.random.key(seed), 3)
    held_modes = noise(splits[0], (HELD, 3, NX, NY, NZ), 1.0, 6.0, ((0, 4), (2, 8)))
    new_modes = noise(splits[1], (NEW, 3, NX, NY, NZ), 1.0, 6.0, ((0, 4), (2, 8)))
    return {"held_modes": held_modes, "new_modes": new_modes}


def gradients(field):
    values = field.astype(jnp.float32)
    along_x = (jnp.roll(values, -1, -3) - jnp.roll(values, 1, -3)) * 0.5
    along_y = (jnp.roll(values, -1, -2) - jnp.roll(values, 1, -2)) * 0.5
    along_z = (jnp.roll(values, -1, -1) - jnp.roll(values, 1, -1)) * 0.5
    return jnp.stack([along_x, along_y, along_z], axis=-4).astype(jnp.bfloat16)

def advect(velocity, grad_block):
    first = velocity[None, :, None, 0].astype(jnp.float32) * grad_block[:, None, :, 0].astype(jnp.float32)
    second = velocity[None, :, None, 1].astype(jnp.float32) * grad_block[:, None, :, 1].astype(jnp.float32)
    third = velocity[None, :, None, 2].astype(jnp.float32) * grad_block[:, None, :, 2].astype(jnp.float32)
    return (first + second + third).astype(jnp.bfloat16)

def reference(held_modes, new_modes):
    cell_count = NX * NY * NZ
    weighting = 1.0 / math.sqrt(NX * NY * NZ)
    every = jnp.concatenate([held_modes, new_modes], 0)
    slopes = gradients(every).reshape(MODES, 3, 3, cell_count)
    velocity = every.reshape(MODES, 3, cell_count)
    all_flat = velocity.reshape(MODES, 3 * cell_count).astype(jnp.float32)
    new_flat = all_flat[HELD:]

    def new_third_one(grad_one):
        advected = advect(velocity, grad_one[None])[0].reshape(MODES, 3 * cell_count)
        return jnp.dot(all_flat, advected.astype(jnp.float32).T, preferred_element_type=jnp.float32) * weighting
    blocks = lax.map(new_third_one, slopes[HELD:])
    new_third = blocks.transpose(1, 0, 2).reshape(MODES, NEW * MODES)

    def held_third_one(grad_one):
        adv_new = advect(velocity[HELD:], grad_one[None])[0].reshape(NEW, 3 * cell_count)
        adv_held = advect(velocity[:HELD], grad_one[None])[0].reshape(HELD, 3 * cell_count)
        onto_all = jnp.dot(all_flat, adv_new.astype(jnp.float32).T, preferred_element_type=jnp.float32) * weighting
        onto_new = jnp.dot(adv_held.astype(jnp.float32), new_flat.T, preferred_element_type=jnp.float32) * weighting
        return (onto_all, onto_new)
    onto_all, onto_new = lax.map(held_third_one, slopes[:HELD])
    held_third_new_second = onto_all[:, :HELD].transpose(1, 0, 2).reshape(HELD, HELD * NEW)
    joined = jnp.concatenate([onto_new, onto_all[:, HELD:].transpose(0, 2, 1)], axis=1)
    held_third_new_first = joined.transpose(1, 0, 2).reshape(MODES, HELD * NEW)
    return (new_third, held_third_new_first, held_third_new_second)
```

```python
import functools
import math

import jax
import jax.numpy as jnp
from jax import lax
from jax.experimental import pallas as pl
from jax.experimental.pallas import tpu as pltpu
from jax.sharding import PartitionSpec as P


F32 = jnp.float32
BF16 = jnp.bfloat16
LANES = 128
NT = (((1,), (1,)), ((), ()))


def shift(count, step):
    return [(i, (i + step) % count) for i in range(count)]


def fill_slopes(before, here, after, slopes):
    comps, _, cells = here.shape
    rows_y = cells // LANES

    def put(entry, y, difference):
        slopes[entry, y] = (difference * 0.5).astype(BF16).astype(F32)

    for a in range(comps):
        line = here[a].astype(F32)
        along_x = after[a].astype(F32) - before[a].astype(F32)
        parts = [line[:, y * LANES : (y + 1) * LANES] for y in range(rows_y)]
        for y in range(rows_y):
            put(a * 3, y, along_x[:, y * LANES : (y + 1) * LANES])
            put(a * 3 + 1, y, parts[(y + 1) % rows_y] - parts[(y - 1) % rows_y])
            put(a * 3 + 2, y, pltpu.roll(parts[y], LANES - 1, 1) - pltpu.roll(parts[y], 1, 1))


def plane_kernel(first, held_own, new_own, blocks, me_ref, before, here, after, *rest):
    sources, rest = rest[:blocks], rest[blocks:]
    totals = None
    if not first:
        totals, rest = rest[:3], rest[3:]
    out_new, out_first, out_second, landed, every, wide, slopes, adv_w, adv_q, adv_n, sems = rest
    step = pl.program_id(0)
    comps, _, cells = here.shape
    held, new = held_own * blocks, new_own * blocks
    total = held + new
    group = total // new
    lines = cells // LANES

    @pl.when(step == 0)
    def _():
        copies = []
        for s, source in enumerate(sources):
            owner = lax.rem(me_ref[0] + blocks - s, blocks)
            copies.append(pltpu.make_async_copy(source, landed.at[owner], sems.at[s]))
        for copy in copies:
            copy.start()
        fill_slopes(before, here, after, slopes)
        for copy in copies:
            copy.wait()
        for owner in range(blocks):
            for a in range(comps):
                block = landed[owner, a].astype(F32)
                columns = slice(a * cells, (a + 1) * cells)
                wide[owner * held_own : (owner + 1) * held_own, columns] = block[:held_own]
                low = held + owner * new_own
                wide[low : low + new_own, columns] = block[held_own:]
        every[...] = wide[...].astype(BF16)

    def slope_rows(k, y, count):
        rows = [slopes[entry, y, pl.ds(k, 8, stride=0), :] for entry in range(3 * comps)]
        return [jnp.concatenate([row] * (count // 8), 0) for row in rows]

    def speeds(low, count, y):
        return [
            wide[low : low + count, a * cells + y * LANES : a * cells + (y + 1) * LANES]
            for a in range(comps)
        ]

    def at(b, y):
        return slice(b * cells + y * LANES, b * cells + (y + 1) * LANES)

    def add(out, which, value):
        out[...] = value if first else value + totals[which][...]

    @pl.when(step < held_own // group)
    def _():
        for kk in range(group):
            rows = slice(kk * new, (kk + 1) * new)
            for y in range(lines):
                g = slope_rows(step * group + kk, y, new)
                v = speeds(held, new, y)
                for b in range(3):
                    adv_w[rows, at(b, y)] = (v[0] * g[b] + v[1] * g[3 + b] + v[2] * g[6 + b]).astype(BF16)
                for a in range(comps):
                    c = 3 * a
                    adv_q[rows, at(a, y)] = (v[0] * g[c] + v[1] * g[c + 1] + v[2] * g[c + 2]).astype(BF16)
        add(out_first, 1, lax.dot_general(every[...], adv_w[...], NT, preferred_element_type=F32))
        add(out_second, 2, lax.dot_general(every[...], adv_q[...], NT, preferred_element_type=F32))

    for y in range(lines):
        g = slope_rows(held_own + step, y, 16)
        for low in range(0, total, 16):
            v = speeds(low, 16, y)
            for b in range(3):
                value = v[0] * g[b] + v[1] * g[3 + b] + v[2] * g[6 + b]
                adv_n[low : low + 16, at(b, y)] = value.astype(BF16)
    add(out_new, 0, lax.dot_general(adv_n[...], every[...], NT, preferred_element_type=F32))


def plane_terms(me, before, here, after, sources, totals, held_own, new_own):
    comps, own, cells = here.shape
    blocks = len(sources)
    total, new, depth = own * blocks, new_own * blocks, comps * cells
    steps = held_own // (total // new)
    whole = pl.BlockSpec((comps, own, cells), lambda t, me: (0, 0, 0))
    tile = pl.BlockSpec((total, total), lambda t, me: (0, t))
    capped = pl.BlockSpec((total, total), lambda t, me: (0, jnp.minimum(t, steps - 1)))
    tiles = [tile, capped, capped]
    in_specs = [whole] * 3 + [pl.BlockSpec(memory_space=pl.ANY)] * blocks
    operands = [before, here, after, *sources]
    aliases = {}
    if totals is not None:
        aliases = {1 + len(operands) + i: i for i in range(3)}
        in_specs += tiles
        operands += totals
    return pl.pallas_call(
        functools.partial(plane_kernel, totals is None, held_own, new_own, blocks),
        out_shape=[
            jax.ShapeDtypeStruct((total, n), F32)
            for n in (new_own * total, held_own * new, held_own * new)
        ],
        grid_spec=pltpu.PrefetchScalarGridSpec(
            num_scalar_prefetch=1,
            grid=(new_own,),
            in_specs=in_specs,
            out_specs=tiles,
            scratch_shapes=[
                pltpu.VMEM((blocks, comps, own, cells), BF16),
                pltpu.VMEM((total, depth), BF16),
                pltpu.VMEM((total, depth), F32),
                pltpu.VMEM((3 * comps, cells // LANES, own, LANES), F32),
                pltpu.VMEM((total, depth), BF16),
                pltpu.VMEM((total, depth), BF16),
                pltpu.VMEM((total, depth), BF16),
                pltpu.SemaphoreType.DMA((blocks,)),
            ],
        ),
        input_output_aliases=aliases,
        compiler_params=pltpu.CompilerParams(
            dimension_semantics=("arbitrary",), vmem_limit_bytes=56 * 2**20
        ),
        name="plane_terms",
    )(me, *operands)


def scatter_sum(parts, order):
    count = lax.axis_size("grid")
    bits = count.bit_length() - 1
    me = lax.axis_index("grid")
    held = parts.reshape((2,) * bits + parts.shape[1:])
    axes = list(range(bits))
    for bit in order:
        axis = axes.index(bits - 1 - bit)
        axes.pop(axis)
        mine = (me >> bit) & 1
        send = lax.dynamic_index_in_dim(held, 1 - mine, axis, keepdims=False)
        keep = lax.dynamic_index_in_dim(held, mine, axis, keepdims=False)
        held = keep + lax.ppermute(send, "grid", [(i, i ^ (1 << bit)) for i in range(count)])
    return held


def per_device(held_modes, new_modes):
    held_own, new_own = held_modes.shape[0], new_modes.shape[0]
    comps, planes = held_modes.shape[1:3]
    cells = held_modes.shape[3] * held_modes.shape[4]
    count, blocks = lax.axis_size("grid"), lax.axis_size("mode")
    weighting = 1.0 / math.sqrt(planes * cells * count)
    own = jnp.concatenate([held_modes, new_modes], 0)
    own = own.transpose(2, 1, 0, 3, 4).reshape(planes, comps, held_own + new_own, cells)
    own = [own[x] for x in range(planes)]
    me = lax.axis_index("mode").astype(jnp.int32).reshape(1)
    padded = [
        lax.ppermute(own[-1], "grid", shift(count, 1)),
        *own,
        lax.ppermute(own[0], "grid", shift(count, -1)),
    ]
    totals = None
    for x in range(planes):
        sources = [own[x]]
        for _ in range(1, blocks):
            sources.append(lax.ppermute(sources[-1], "mode", shift(blocks, 1)))
        totals = plane_terms(
            me, padded[x], padded[x + 1], padded[x + 2], sources, totals, held_own, new_own
        )
    bits = count.bit_length() - 1
    orders = ([0, *range(1, bits)], [0, *range(bits - 1, 0, -1)])
    held = held_own * blocks
    results = []
    for which, value in enumerate(totals):
        rows = held if which == 2 else value.shape[0]
        parts = value[:rows].reshape(count, rows // count, value.shape[1])
        half = value.shape[1] // 2
        results.append(
            jnp.concatenate(
                [scatter_sum(parts[:, :, :half], orders[0]), scatter_sum(parts[:, :, half:], orders[1])], 1
            )
            * weighting
        )
    return tuple(results)


def solution(mesh):
    placed = (P("mode", None, "grid", None, None), P("mode", None, "grid", None, None))
    return jax.shard_map(
        per_device,
        mesh=mesh,
        in_specs=placed,
        out_specs=(P("grid", "mode"), P("grid", "mode"), P("grid", "mode")),
        check_vma=False,
    )
```

```python
import functools
import math

import jax
import jax.numpy as jnp
from jax import lax
from jax.experimental import pallas as pl
from jax.experimental.pallas import tpu as pltpu
from jax.sharding import PartitionSpec as P


F32 = jnp.float32
BF16 = jnp.bfloat16
LANES = 128
NT = (((1,), (1,)), ((), ()))


def shift(count, step):
    return [(i, (i + step) % count) for i in range(count)]


def fill_slopes(before, here, after, slopes):
    comps, _, cells = here.shape
    rows_y = cells // LANES

    def put(entry, y, difference):
        slopes[entry, y] = (difference * 0.5).astype(BF16).astype(F32)

    for a in range(comps):
        line = here[a].astype(F32)
        along_x = after[a].astype(F32) - before[a].astype(F32)
        parts = [line[:, y * LANES : (y + 1) * LANES] for y in range(rows_y)]
        for y in range(rows_y):
            put(a * 3, y, along_x[:, y * LANES : (y + 1) * LANES])
            put(a * 3 + 1, y, parts[(y + 1) % rows_y] - parts[(y - 1) % rows_y])
            put(a * 3 + 2, y, pltpu.roll(parts[y], LANES - 1, 1) - pltpu.roll(parts[y], 1, 1))


def plane_kernel(first, held_own, new_own, owners, blocks, me_ref, before, here, after, *rest):
    sources, rest = rest[:blocks], rest[blocks:]
    totals = None
    if not first:
        totals, rest = rest[0], rest[1:]
    out, rest = rest[0], rest[1:]
    every, every_held, wide, slopes, even, odd = rest
    comps, _, cells = here.shape
    held, new = held_own * blocks, new_own * blocks
    total = held + new
    group = total // new
    steps = held_own // group
    lines = cells // LANES
    half = total // 2

    fill_slopes(before, here, after, slopes)
    for s, source in enumerate(sources):
        owner = lax.rem(me_ref[0] + blocks - s, blocks)
        low = pl.multiple_of(owner * held_own, 8)
        low_new = pl.multiple_of(held + owner * new_own, 8)
        for a in range(comps):
            block = source[a].astype(F32)
            columns = slice(a * cells, (a + 1) * cells)
            wide[pl.ds(low, held_own), columns] = block[:held_own]
            wide[pl.ds(low_new, new_own), columns] = block[held_own:]

    def by_owner(target, count):
        rows = total // owners
        for parity in range(2):
            start = pl.multiple_of(jnp.where(me_ref[1] == parity, 0, half), half)
            for low in range(0, comps * cells, LANES):
                columns = slice(low, low + LANES)
                parts = [
                    wide[g * count // owners : g * count // owners + rows, columns]
                    for g in range(parity, owners, 2)
                ]
                target[pl.ds(start, half), columns] = jnp.concatenate(parts, 0).astype(BF16)

    by_owner(every, total)
    by_owner(every_held, held)

    def slope_rows(k, y, count):
        rows = [slopes[entry, y, pl.ds(k, 8, stride=0), :] for entry in range(3 * comps)]
        return [jnp.concatenate([row] * (count // 8), 0) for row in rows]

    def at(b, y):
        return slice(b * cells + y * LANES, b * cells + (y + 1) * LANES)

    def speeds(low, count, y):
        return [wide[low : low + count, at(a, y)] for a in range(comps)]

    def along(v, g, terms):
        return (v[0] * g[terms[0]] + v[1] * g[terms[1]] + v[2] * g[terms[2]]).astype(BF16)

    def fill_mixed(buffer, step):
        for y in range(lines):
            v = speeds(held, new, y)
            for kk in range(group):
                g = slope_rows(step * group + kk, y, new)
                low = kk * new
                for b in range(3):
                    buffer[low : low + new, at(b, y)] = along(v, g, (b, 3 + b, 6 + b))
                low += 2 * total
                for a in range(comps):
                    value = along(v, g, (3 * a, 3 * a + 1, 3 * a + 2))
                    buffer[low : low + new, at(a, y)] = value

    def fill_new(buffer, base, step):
        for y in range(lines):
            g = slope_rows(held_own + step, y, 16)
            for low in range(0, total, 16):
                v = speeds(low, 16, y)
                for a in range(comps):
                    value = along(v, g, (3 * a, 3 * a + 1, 3 * a + 2))
                    buffer[base + low : base + low + 16, at(a, y)] = value

    def fill(buffer, step):
        fill_mixed(buffer, step)
        fill_new(buffer, total, step)

    def add(tile, value):
        columns = pl.ds(pl.multiple_of(tile * total, LANES), total)
        out[:, columns] = value if first else totals[:, columns] + value

    def product(rows, buffer, low, count):
        return lax.dot_general(rows[...], buffer[low : low + count, :], NT, preferred_element_type=F32)

    def flush(buffer, step):
        value = product(every, buffer, 0, 2 * total)
        add(new_own + step, value[:, :total])
        add(step, value[:, total:])
        add(new_own + steps + step, product(every_held, buffer, 2 * total, total))

    fill(even, 0)

    def pair(i, carry):
        fill(odd, 2 * i + 1)
        flush(even, 2 * i)
        fill(even, 2 * i + 2)
        flush(odd, 2 * i + 1)
        return carry

    lax.fori_loop(0, (steps - 1) // 2, pair, 0)
    buffers = [even, odd]
    for step in range((steps - 1) // 2 * 2 + 1, steps):
        fill(buffers[step % 2], step)
        flush(buffers[(step - 1) % 2], step - 1)
    spare = buffers[steps % 2]
    for step in range(steps, new_own):
        fill_new(spare, (step - steps) * total, step)
    flush(buffers[(steps - 1) % 2], steps - 1)
    for step in range(steps, new_own):
        add(step, product(every, spare, (step - steps) * total, total))


def plane_terms(place, before, here, after, sources, totals, held_own, new_own, owners):
    comps, own, cells = here.shape
    blocks = len(sources)
    total, new, depth = own * blocks, new_own * blocks, comps * cells
    vmem = pl.BlockSpec(memory_space=pltpu.VMEM)
    operands = [place, before, here, after, *sources]
    aliases = {}
    if totals is not None:
        aliases = {len(operands): 0}
        operands.append(totals)
    columns = new_own * total + 2 * held_own * new
    vmem_mib = 16
    return pl.pallas_call(
        functools.partial(plane_kernel, totals is None, held_own, new_own, owners, blocks),
        out_shape=jax.ShapeDtypeStruct((total, columns), F32),
        in_specs=[pl.BlockSpec(memory_space=pltpu.SMEM)] + [vmem] * (len(operands) - 1),
        out_specs=vmem,
        scratch_shapes=[
            pltpu.VMEM((total, depth), BF16),
            pltpu.VMEM((total, depth), BF16),
            pltpu.VMEM((total, depth), F32),
            pltpu.VMEM((3 * comps, cells // LANES, own, LANES), F32),
            pltpu.VMEM((3 * total, depth), BF16),
            pltpu.VMEM((3 * total, depth), BF16),
        ],
        input_output_aliases=aliases,
        compiler_params=pltpu.CompilerParams(vmem_limit_bytes=vmem_mib * 2**20),
        name="plane_terms",
    )(*operands)


def scatter_sum(held, order):
    count = lax.axis_size("grid")
    bits = count.bit_length() - 1
    me = lax.axis_index("grid")
    left = list(range(bits - 1, 0, -1))
    for bit in order:
        axis = left.index(bit)
        left.pop(axis)
        mine = (me >> bit) & 1
        send = lax.dynamic_index_in_dim(held, 1 - mine, axis, keepdims=False).astype(BF16)
        keep = lax.dynamic_index_in_dim(held, mine, axis, keepdims=False)
        held = keep + lax.ppermute(send, "grid", [(i, i ^ (1 << bit)) for i in range(count)]).astype(F32)
    return held


def per_device(held_modes, new_modes):
    held_own, new_own = held_modes.shape[0], new_modes.shape[0]
    comps, planes = held_modes.shape[1:3]
    cells = held_modes.shape[3] * held_modes.shape[4]
    count, blocks = lax.axis_size("grid"), lax.axis_size("mode")
    bits = count.bit_length() - 1
    weighting = 1.0 / math.sqrt(planes * cells * count)
    own = jnp.concatenate([held_modes, new_modes], 0)
    own = own.transpose(2, 1, 0, 3, 4).reshape(planes, comps, held_own + new_own, cells)
    own = [own[x] for x in range(planes)]
    place = jnp.stack([lax.axis_index("mode"), lax.axis_index("grid") & 1]).astype(jnp.int32)
    padded = [
        lax.ppermute(own[-1], "grid", shift(count, 1)),
        *own,
        lax.ppermute(own[0], "grid", shift(count, -1)),
    ]
    totals = None
    for x in range(planes):
        sources = [lax.ppermute(own[x], "mode", shift(blocks, s)) if s else own[x] for s in range(blocks)]
        totals = plane_terms(
            place, padded[x], padded[x + 1], padded[x + 2], sources, totals, held_own, new_own, count
        )
    half = totals.shape[0] // 2
    sums = totals[:half] + lax.ppermute(totals[half:], "grid", [(i, i ^ 1) for i in range(count)])
    sums = sums.reshape((2,) * (bits - 1) + (-1, sums.shape[1]))
    middle = sums.shape[-1] // 2
    mine = jnp.concatenate(
        [
            scatter_sum(sums[..., :middle], list(range(1, bits))),
            scatter_sum(sums[..., middle:], list(range(bits - 1, 0, -1))),
        ],
        1,
    ) * weighting
    new_third = new_own * (held_own + new_own) * blocks
    held_third = held_own * new_own * blocks
    return (
        mine[:, :new_third],
        mine[:, new_third : new_third + held_third],
        mine[: held_own * blocks // count, new_third + held_third :],
    )


def solution(mesh):
    placed = (P("mode", None, "grid", None, None), P("mode", None, "grid", None, None))
    return jax.shard_map(
        per_device,
        mesh=mesh,
        in_specs=placed,
        out_specs=(P("grid", "mode"), P("grid", "mode"), P("grid", "mode")),
        check_vma=False,
    )
```

```python
import functools
import math

import jax
import jax.numpy as jnp
from jax import lax
from jax.experimental import pallas as pl
from jax.experimental.pallas import tpu as pltpu
from jax.sharding import PartitionSpec as P


F32 = jnp.float32
BF16 = jnp.bfloat16
LANES = 128
NT = (((1,), (1,)), ((), ()))


def shift(count, step):
    return [(i, (i + step) % count) for i in range(count)]


def fill_slopes(before, here, after, slopes):
    comps, _, cells = here.shape
    rows_y = cells // LANES

    def put(entry, y, difference):
        slopes[entry, y] = (difference * 0.5).astype(BF16).astype(F32)

    for a in range(comps):
        line = here[a].astype(F32)
        along_x = after[a].astype(F32) - before[a].astype(F32)
        parts = [line[:, y * LANES : (y + 1) * LANES] for y in range(rows_y)]
        for y in range(rows_y):
            put(a * 3, y, along_x[:, y * LANES : (y + 1) * LANES])
            put(a * 3 + 1, y, parts[(y + 1) % rows_y] - parts[(y - 1) % rows_y])
            put(a * 3 + 2, y, pltpu.roll(parts[y], LANES - 1, 1) - pltpu.roll(parts[y], 1, 1))


def plane_kernel(first, last, held_own, new_own, owners, blocks, me_ref, before, here, after, *rest):
    sources, rest = rest[:blocks], rest[blocks:]
    totals = None
    if not first:
        totals, rest = rest[0], rest[1:]
    outs, rest = rest[: 1 + last], rest[1 + last :]
    every, every_held, wide, slopes, fill_a, fill_b, fill_c = rest
    comps, _, cells = here.shape
    held, new = held_own * blocks, new_own * blocks
    total = held + new
    group = total // new
    steps = held_own // group
    lines = cells // LANES
    half = total // 2

    fill_slopes(before, here, after, slopes)
    for s, source in enumerate(sources):
        owner = lax.rem(me_ref[0] + blocks - s, blocks)
        low = pl.multiple_of(owner * held_own, 8)
        low_new = pl.multiple_of(held + owner * new_own, 8)
        for a in range(comps):
            block = source[a].astype(F32)
            columns = slice(a * cells, (a + 1) * cells)
            wide[pl.ds(low, held_own), columns] = block[:held_own]
            wide[pl.ds(low_new, new_own), columns] = block[held_own:]

    def by_owner(target, count):
        rows = total // owners
        for parity in range(2):
            start = pl.multiple_of(jnp.where(me_ref[1] == parity, 0, half), half)
            for low in range(0, comps * cells, LANES):
                columns = slice(low, low + LANES)
                parts = [
                    wide[g * count // owners : g * count // owners + rows, columns]
                    for g in range(parity, owners, 2)
                ]
                target[pl.ds(start, half), columns] = jnp.concatenate(parts, 0).astype(BF16)

    by_owner(every, total)
    by_owner(every_held, held)

    def slope_rows(k, y, count):
        rows = [slopes[entry, y, pl.ds(k, 8, stride=0), :] for entry in range(3 * comps)]
        return [jnp.concatenate([row] * (count // 8), 0) for row in rows]

    def at(b, y):
        return slice(b * cells + y * LANES, b * cells + (y + 1) * LANES)

    def speeds(low, count, y):
        return [wide[low : low + count, at(a, y)] for a in range(comps)]

    def along(v, g, terms):
        return (v[0] * g[terms[0]] + v[1] * g[terms[1]] + v[2] * g[terms[2]]).astype(BF16)

    def fill_held(buffer, step, entries):
        for y in range(lines):
            for kk in range(group):
                g = slope_rows(step * group + kk, y, 16)
                for part in range(0, new, 16):
                    v = speeds(held + part, 16, y)
                    low = kk * new + part
                    for c in range(3):
                        buffer[low : low + 16, at(c, y)] = along(v, g, entries(c))

    def fill_new(buffer, step, entries):
        for y in range(lines):
            g = slope_rows(held_own + step, y, 16)
            for low in range(0, total, 16):
                v = speeds(low, 16, y)
                for c in range(3):
                    buffer[low : low + 16, at(c, y)] = along(v, g, entries(c))

    def onto_first(c):
        return (c, 3 + c, 6 + c)

    def onto_second(c):
        return (3 * c, 3 * c + 1, 3 * c + 2)

    def add(tile, rows, buffer):
        value = lax.dot_general(rows[...], buffer[...], NT, preferred_element_type=F32)
        columns = pl.ds(pl.multiple_of(tile * total, LANES), total)
        value = value if first else totals[:, columns] + value
        for i, out in enumerate(outs):
            out[:, columns] = value[i * half : (i + 1) * half] if last else value

    def one(step, carry):
        @pl.when(step == 0)
        def _():
            fill_new(fill_a, step, onto_second)

        @pl.when(step > 0)
        def _():
            fill_new(fill_a, step, onto_second)
            add(new_own + steps + step - 1, every_held, fill_c)

        @pl.when(step < steps)
        def _():
            fill_held(fill_b, step, onto_first)
            add(step, every, fill_a)

        @pl.when(step < steps)
        def _():
            fill_held(fill_c, step, onto_second)
            add(new_own + step, every, fill_b)

        @pl.when(step >= steps)
        def _():
            add(step, every, fill_a)

        return carry

    lax.fori_loop(0, new_own, one, 0)


def plane_terms(place, before, here, after, sources, totals, last, held_own, new_own, owners):
    comps, own, cells = here.shape
    blocks = len(sources)
    total, new, depth = own * blocks, new_own * blocks, comps * cells
    vmem = pl.BlockSpec(memory_space=pltpu.VMEM)
    operands = [place, before, here, after, *sources]
    aliases = {}
    if totals is not None:
        aliases = {} if last else {len(operands): 0}
        operands.append(totals)
    columns = new_own * total + 2 * held_own * new
    vmem_mib = 16
    rows = [total // 2] * 2 if last else [total]
    return pl.pallas_call(
        functools.partial(plane_kernel, totals is None, last, held_own, new_own, owners, blocks),
        out_shape=[jax.ShapeDtypeStruct((n, columns), F32) for n in rows],
        in_specs=[pl.BlockSpec(memory_space=pltpu.SMEM)] + [vmem] * (len(operands) - 1),
        out_specs=[vmem] * len(rows),
        scratch_shapes=[
            pltpu.VMEM((total, depth), BF16),
            pltpu.VMEM((total, depth), BF16),
            pltpu.VMEM((total, depth), F32),
            pltpu.VMEM((3 * comps, cells // LANES, own, LANES), F32),
            pltpu.VMEM((total, depth), BF16),
            pltpu.VMEM((total, depth), BF16),
            pltpu.VMEM((total, depth), BF16),
        ],
        input_output_aliases=aliases,
        compiler_params=pltpu.CompilerParams(vmem_limit_bytes=vmem_mib * 2**20),
        name="plane_terms",
    )(*operands)


def scatter_sum(held, order):
    count = lax.axis_size("grid")
    bits = count.bit_length() - 1
    me = lax.axis_index("grid")
    left = list(range(bits - 1, 0, -1))
    for bit in order:
        axis = left.index(bit)
        left.pop(axis)
        mine = (me >> bit) & 1
        send = lax.dynamic_index_in_dim(held, 1 - mine, axis, keepdims=False).astype(BF16)
        keep = lax.dynamic_index_in_dim(held, mine, axis, keepdims=False)
        held = keep + lax.ppermute(send, "grid", [(i, i ^ (1 << bit)) for i in range(count)]).astype(F32)
    return held


def gather_planes(own, blocks):
    arrived = []
    for x, plane in enumerate(own):
        here, back = plane, plane
        if x >= 2:
            here, _ = lax.optimization_barrier((plane, arrived[x - 2][1]))
        if x >= 1:
            back, _ = lax.optimization_barrier((plane, arrived[x - 1][1]))
        parts = [plane, lax.ppermute(here, "mode", shift(blocks, 1))]
        end = lax.ppermute(back, "mode", shift(blocks, -1))
        while len(parts) < blocks - 1:
            parts.append(lax.ppermute(parts[-1], "mode", shift(blocks, 1)))
        arrived.append(parts + [end])
    return arrived


def per_device(held_modes, new_modes):
    held_own, new_own = held_modes.shape[0], new_modes.shape[0]
    comps, planes = held_modes.shape[1:3]
    cells = held_modes.shape[3] * held_modes.shape[4]
    count, blocks = lax.axis_size("grid"), lax.axis_size("mode")
    bits = count.bit_length() - 1
    weighting = 1.0 / math.sqrt(planes * cells * count)
    own = jnp.concatenate([held_modes, new_modes], 0)
    own = own.transpose(2, 1, 0, 3, 4).reshape(planes, comps, held_own + new_own, cells)
    own = [own[x] for x in range(planes)]
    place = jnp.stack([lax.axis_index("mode"), lax.axis_index("grid") & 1]).astype(jnp.int32)
    padded = [
        lax.ppermute(own[-1], "grid", shift(count, 1)),
        *own,
        lax.ppermute(own[0], "grid", shift(count, -1)),
    ]
    arrived = gather_planes(own, blocks)
    totals = None
    for x in range(planes):
        last = x == planes - 1
        around = padded[x : x + 3]
        ends = plane_terms(place, *around, arrived[x], totals, last, held_own, new_own, count)
        totals = ends[0]
    keep, send = ends
    sums = keep + lax.ppermute(send, "grid", [(i, i ^ 1) for i in range(count)])
    sums = sums.reshape((2,) * (bits - 1) + (-1, sums.shape[1]))
    middle = sums.shape[-1] // 2 // LANES * LANES
    left = scatter_sum(sums[..., :middle], list(range(1, bits))) * weighting
    right = scatter_sum(sums[..., middle:], list(range(bits - 1, 0, -1))) * weighting
    new_third = new_own * (held_own + new_own) * blocks
    held_third = held_own * new_own * blocks
    rest = new_third + held_third - middle
    return (
        left[:, :new_third],
        jnp.concatenate([left[:, new_third:], right[:, :rest]], 1),
        right[: held_own * blocks // count, rest:],
    )


def solution(mesh):
    placed = (P("mode", None, "grid", None, None), P("mode", None, "grid", None, None))
    return jax.shard_map(
        per_device,
        mesh=mesh,
        in_specs=placed,
        out_specs=(P("grid", "mode"), P("grid", "mode"), P("grid", "mode")),
        check_vma=False,
    )
```

```python
import functools
import math

import jax
import jax.numpy as jnp
from jax import lax
from jax.experimental import pallas as pl
from jax.experimental.pallas import tpu as pltpu
from jax.sharding import PartitionSpec as P


F32 = jnp.float32
BF16 = jnp.bfloat16
LANES = 128
NT = (((1,), (1,)), ((), ()))


def shift(count, step):
    return [(i, (i + step) % count) for i in range(count)]


def fill_slopes(before, here, after, slopes):
    comps, _, cells = here.shape
    rows_y = cells // LANES

    def put(entry, y, difference):
        slopes[entry, y] = (difference * 0.5).astype(BF16).astype(F32)

    for a in range(comps):
        line = here[a].astype(F32)
        along_x = after[a].astype(F32) - before[a].astype(F32)
        parts = [line[:, y * LANES : (y + 1) * LANES] for y in range(rows_y)]
        for y in range(rows_y):
            put(a * 3, y, along_x[:, y * LANES : (y + 1) * LANES])
            put(a * 3 + 1, y, parts[(y + 1) % rows_y] - parts[(y - 1) % rows_y])
            put(a * 3 + 2, y, pltpu.roll(parts[y], LANES - 1, 1) - pltpu.roll(parts[y], 1, 1))


def plane_kernel(first, last, held_own, new_own, owners, blocks, me_ref, before, here, after, *rest):
    sources, rest = rest[:blocks], rest[blocks:]
    totals = None
    if not first:
        totals, rest = rest[0], rest[1:]
    outs, rest = rest[: 1 + last], rest[1 + last :]
    every, every_held, wide, slopes, fill_a, fill_b, fill_c = rest
    comps, _, cells = here.shape
    held, new = held_own * blocks, new_own * blocks
    total = held + new
    group = total // new
    steps = held_own // group
    lines = cells // LANES
    half = total // 2

    fill_slopes(before, here, after, slopes)
    for s, source in enumerate(sources):
        owner = lax.rem(me_ref[0] + blocks - s, blocks)
        low = pl.multiple_of(owner * held_own, 8)
        low_new = pl.multiple_of(held + owner * new_own, 8)
        for a in range(comps):
            block = source[a].astype(F32)
            columns = slice(a * cells, (a + 1) * cells)
            wide[pl.ds(low, held_own), columns] = block[:held_own]
            wide[pl.ds(low_new, new_own), columns] = block[held_own:]

    def by_owner(target, count):
        rows = total // owners
        for parity in range(2):
            start = pl.multiple_of(jnp.where(me_ref[1] == parity, 0, half), half)
            for low in range(0, comps * cells, LANES):
                columns = slice(low, low + LANES)
                parts = [
                    wide[g * count // owners : g * count // owners + rows, columns]
                    for g in range(parity, owners, 2)
                ]
                target[pl.ds(start, half), columns] = jnp.concatenate(parts, 0).astype(BF16)

    by_owner(every, total)
    by_owner(every_held, held)

    def slope_rows(k, y, count):
        rows = [slopes[entry, y, pl.ds(k, 8, stride=0), :] for entry in range(3 * comps)]
        return [jnp.concatenate([row] * (count // 8), 0) for row in rows]

    def at(b, y):
        return slice(b * cells + y * LANES, b * cells + (y + 1) * LANES)

    def speeds(low, count, y):
        return [wide[low : low + count, at(a, y)] for a in range(comps)]

    def along(v, g, terms):
        return (v[0] * g[terms[0]] + v[1] * g[terms[1]] + v[2] * g[terms[2]]).astype(BF16)

    def fill_held(buffer, step, entries):
        for y in range(lines):
            for kk in range(group):
                g = slope_rows(step * group + kk, y, 16)
                for part in range(0, new, 16):
                    v = speeds(held + part, 16, y)
                    low = kk * new + part
                    for c in range(3):
                        buffer[low : low + 16, at(c, y)] = along(v, g, entries(c))

    def fill_new(buffer, step, entries):
        for y in range(lines):
            g = slope_rows(held_own + step, y, 16)
            for low in range(0, total, 16):
                v = speeds(low, 16, y)
                for c in range(3):
                    buffer[low : low + 16, at(c, y)] = along(v, g, entries(c))

    def onto_first(c):
        return (c, 3 + c, 6 + c)

    def onto_second(c):
        return (3 * c, 3 * c + 1, 3 * c + 2)

    def add(tile, rows, buffer):
        value = lax.dot_general(rows[...], buffer[...], NT, preferred_element_type=F32)
        columns = pl.ds(pl.multiple_of(tile * total, LANES), total)
        value = value if first else totals[:, columns] + value
        for i, out in enumerate(outs):
            out[:, columns] = value[i * half : (i + 1) * half] if last else value

    def one(step, carry):
        @pl.when(step == 0)
        def _():
            fill_new(fill_a, step, onto_second)

        @pl.when(step > 0)
        def _():
            fill_new(fill_a, step, onto_second)
            add(new_own + steps + step - 1, every_held, fill_c)

        @pl.when(step < steps)
        def _():
            fill_held(fill_b, step, onto_first)
            add(step, every, fill_a)

        @pl.when(step < steps)
        def _():
            fill_held(fill_c, step, onto_second)
            add(new_own + step, every, fill_b)

        @pl.when(step >= steps)
        def _():
            add(step, every, fill_a)

        return carry

    lax.fori_loop(0, new_own, one, 0)


def plane_terms(place, before, here, after, sources, totals, last, held_own, new_own, owners):
    comps, own, cells = here.shape
    blocks = len(sources)
    total, new, depth = own * blocks, new_own * blocks, comps * cells
    vmem = pl.BlockSpec(memory_space=pltpu.VMEM)
    operands = [place, before, here, after, *sources]
    aliases = {}
    if totals is not None:
        aliases = {} if last else {len(operands): 0}
        operands.append(totals)
    columns = new_own * total + 2 * held_own * new
    vmem_mib = 16
    rows = [total // 2] * 2 if last else [total]
    return pl.pallas_call(
        functools.partial(plane_kernel, totals is None, last, held_own, new_own, owners, blocks),
        out_shape=[jax.ShapeDtypeStruct((n, columns), F32) for n in rows],
        in_specs=[pl.BlockSpec(memory_space=pltpu.SMEM)] + [vmem] * (len(operands) - 1),
        out_specs=[vmem] * len(rows),
        scratch_shapes=[
            pltpu.VMEM((total, depth), BF16),
            pltpu.VMEM((total, depth), BF16),
            pltpu.VMEM((total, depth), F32),
            pltpu.VMEM((3 * comps, cells // LANES, own, LANES), F32),
            pltpu.VMEM((total, depth), BF16),
            pltpu.VMEM((total, depth), BF16),
            pltpu.VMEM((total, depth), BF16),
        ],
        input_output_aliases=aliases,
        compiler_params=pltpu.CompilerParams(vmem_limit_bytes=vmem_mib * 2**20),
        name="plane_terms",
    )(*operands)


def scatter_sum(held, order):
    count = lax.axis_size("grid")
    bits = count.bit_length() - 1
    me = lax.axis_index("grid")
    left = list(range(bits - 1, 0, -1))
    for bit in order:
        axis = left.index(bit)
        left.pop(axis)
        mine = (me >> bit) & 1
        send = lax.dynamic_index_in_dim(held, 1 - mine, axis, keepdims=False).astype(BF16)
        keep = lax.dynamic_index_in_dim(held, mine, axis, keepdims=False)
        held = keep + lax.ppermute(send, "grid", [(i, i ^ (1 << bit)) for i in range(count)]).astype(F32)
    return held


def gather_planes(own, blocks):
    arrived = []
    for plane in own:
        parts = [plane]
        for s in range(1, blocks):
            straight = s == blocks - 1
            source = plane if straight else parts[-1]
            parts.append(lax.ppermute(source, "mode", shift(blocks, -1 if straight else 1)))
        arrived.append(parts)
    return arrived


def per_device(held_modes, new_modes):
    held_own, new_own = held_modes.shape[0], new_modes.shape[0]
    comps, planes = held_modes.shape[1:3]
    cells = held_modes.shape[3] * held_modes.shape[4]
    count, blocks = lax.axis_size("grid"), lax.axis_size("mode")
    bits = count.bit_length() - 1
    weighting = 1.0 / math.sqrt(planes * cells * count)
    own = jnp.concatenate([held_modes, new_modes], 0)
    own = own.transpose(2, 1, 0, 3, 4).reshape(planes, comps, held_own + new_own, cells)
    own = [own[x] for x in range(planes)]
    place = jnp.stack([lax.axis_index("mode"), lax.axis_index("grid") & 1]).astype(jnp.int32)
    padded = [
        lax.ppermute(own[-1], "grid", shift(count, 1)),
        *own,
        lax.ppermute(own[0], "grid", shift(count, -1)),
    ]
    arrived = gather_planes(own, blocks)
    totals = None
    for x in range(planes):
        last = x == planes - 1
        around = padded[x : x + 3]
        ends = plane_terms(place, *around, arrived[x], totals, last, held_own, new_own, count)
        totals = ends[0]
    keep, send = ends
    sums = keep + lax.ppermute(send, "grid", [(i, i ^ 1) for i in range(count)])
    sums = sums.reshape((2,) * (bits - 1) + (-1, sums.shape[1]))
    middle = sums.shape[-1] // 2 // LANES * LANES
    left = scatter_sum(sums[..., :middle], list(range(1, bits))) * weighting
    right = scatter_sum(sums[..., middle:], list(range(bits - 1, 0, -1))) * weighting
    new_third = new_own * (held_own + new_own) * blocks
    held_third = held_own * new_own * blocks
    rest = new_third + held_third - middle
    return (
        left[:, :new_third],
        jnp.concatenate([left[:, new_third:], right[:, :rest]], 1),
        right[: held_own * blocks // count, rest:],
    )


def solution(mesh):
    placed = (P("mode", None, "grid", None, None), P("mode", None, "grid", None, None))

    def step(held_modes, new_modes):
        body = jax.shard_map(
            per_device,
            mesh=mesh,
            in_specs=placed,
            out_specs=(P("grid", "mode"), P("grid", "mode"), P("grid", "mode")),
            check_vma=False,
        )
        return body(held_modes, new_modes)

    return step
```

```python
import functools
import math

import jax
import jax.numpy as jnp
from jax import lax
from jax.experimental import pallas as pl
from jax.experimental.pallas import tpu as pltpu
from jax.sharding import PartitionSpec as P


F32 = jnp.float32
BF16 = jnp.bfloat16
LANES = 128
NT = (((1,), (1,)), ((), ()))


def shift(count, step):
    return [(i, (i + step) % count) for i in range(count)]


def fill_slopes(before, here, after, slopes):
    comps, _, cells = here.shape
    rows_y = cells // LANES

    def put(entry, y, difference):
        slopes[entry, y] = (difference * 0.5).astype(BF16).astype(F32)

    for a in range(comps):
        line = here[a].astype(F32)
        along_x = after[a].astype(F32) - before[a].astype(F32)
        parts = [line[:, y * LANES : (y + 1) * LANES] for y in range(rows_y)]
        for y in range(rows_y):
            put(a * 3, y, along_x[:, y * LANES : (y + 1) * LANES])
            put(a * 3 + 1, y, parts[(y + 1) % rows_y] - parts[(y - 1) % rows_y])
            put(a * 3 + 2, y, pltpu.roll(parts[y], LANES - 1, 1) - pltpu.roll(parts[y], 1, 1))


def plane_kernel(first, last, held_own, new_own, owners, blocks, me_ref, before, here, after, *rest):
    sources, rest = rest[:blocks], rest[blocks:]
    totals = None
    if not first:
        totals, rest = rest[0], rest[1:]
    outs, rest = rest[: 1 + last], rest[1 + last :]
    every, every_held, wide, slopes, fill_a, fill_b, fill_c = rest
    comps, _, cells = here.shape
    held, new = held_own * blocks, new_own * blocks
    total = held + new
    group = total // new
    steps = held_own // group
    lines = cells // LANES
    half = total // 2

    fill_slopes(before, here, after, slopes)
    for s, source in enumerate(sources):
        owner = lax.rem(me_ref[0] + blocks - s, blocks)
        low = pl.multiple_of(owner * held_own, 8)
        low_new = pl.multiple_of(held + owner * new_own, 8)
        for a in range(comps):
            block = source[a].astype(F32)
            columns = slice(a * cells, (a + 1) * cells)
            wide[pl.ds(low, held_own), columns] = block[:held_own]
            wide[pl.ds(low_new, new_own), columns] = block[held_own:]

    def by_owner(target, count):
        rows = total // owners
        for parity in range(2):
            start = pl.multiple_of(jnp.where(me_ref[1] == parity, 0, half), half)
            for low in range(0, comps * cells, LANES):
                columns = slice(low, low + LANES)
                parts = [
                    wide[g * count // owners : g * count // owners + rows, columns]
                    for g in range(parity, owners, 2)
                ]
                target[pl.ds(start, half), columns] = jnp.concatenate(parts, 0).astype(BF16)

    by_owner(every, total)
    by_owner(every_held, held)

    def slope_rows(k, y, count):
        rows = [slopes[entry, y, pl.ds(k, 8, stride=0), :] for entry in range(3 * comps)]
        return [jnp.concatenate([row] * (count // 8), 0) for row in rows]

    def at(b, y):
        return slice(b * cells + y * LANES, b * cells + (y + 1) * LANES)

    def speeds(low, count, y):
        return [wide[low : low + count, at(a, y)] for a in range(comps)]

    def along(v, g, terms):
        return (v[0] * g[terms[0]] + v[1] * g[terms[1]] + v[2] * g[terms[2]]).astype(BF16)

    def fill_held(buffer, step, entries):
        for y in range(lines):
            for kk in range(group):
                g = slope_rows(step * group + kk, y, 16)
                for part in range(0, new, 16):
                    v = speeds(held + part, 16, y)
                    low = kk * new + part
                    for c in range(3):
                        buffer[low : low + 16, at(c, y)] = along(v, g, entries(c))

    def fill_new(buffer, step, entries):
        for y in range(lines):
            g = slope_rows(held_own + step, y, 16)
            for low in range(0, total, 16):
                v = speeds(low, 16, y)
                for c in range(3):
                    buffer[low : low + 16, at(c, y)] = along(v, g, entries(c))

    def onto_first(c):
        return (c, 3 + c, 6 + c)

    def onto_second(c):
        return (3 * c, 3 * c + 1, 3 * c + 2)

    def add(tile, rows, buffer):
        value = lax.dot_general(rows[...], buffer[...], NT, preferred_element_type=F32)
        columns = pl.ds(pl.multiple_of(tile * total, LANES), total)
        value = value if first else totals[:, columns] + value
        for i, out in enumerate(outs):
            out[:, columns] = value[i * half : (i + 1) * half].astype(out.dtype) if last else value

    def one(step, carry):
        @pl.when(step == 0)
        def _():
            fill_new(fill_a, step, onto_second)

        @pl.when(step > 0)
        def _():
            fill_new(fill_a, step, onto_second)
            add(new_own + steps + step - 1, every_held, fill_c)

        @pl.when(step < steps)
        def _():
            fill_held(fill_b, step, onto_first)
            add(step, every, fill_a)

        @pl.when(step < steps)
        def _():
            fill_held(fill_c, step, onto_second)
            add(new_own + step, every, fill_b)

        @pl.when(step >= steps)
        def _():
            add(step, every, fill_a)

        return carry

    lax.fori_loop(0, new_own, one, 0)


def plane_terms(place, before, here, after, sources, totals, last, held_own, new_own, owners):
    comps, own, cells = here.shape
    blocks = len(sources)
    total, new, depth = own * blocks, new_own * blocks, comps * cells
    vmem = pl.BlockSpec(memory_space=pltpu.VMEM)
    operands = [place, before, here, after, *sources]
    aliases = {}
    if totals is not None:
        aliases = {} if last else {len(operands): 0}
        operands.append(totals)
    columns = new_own * total + 2 * held_own * new
    vmem_mib = 16
    rows = [total // 2] * 2 if last else [total]
    return pl.pallas_call(
        functools.partial(plane_kernel, totals is None, last, held_own, new_own, owners, blocks),
        out_shape=[jax.ShapeDtypeStruct((n, columns), t) for n, t in zip(rows, (F32, BF16))],
        in_specs=[pl.BlockSpec(memory_space=pltpu.SMEM)] + [vmem] * (len(operands) - 1),
        out_specs=[vmem] * len(rows),
        scratch_shapes=[
            pltpu.VMEM((total, depth), BF16),
            pltpu.VMEM((total, depth), BF16),
            pltpu.VMEM((total, depth), F32),
            pltpu.VMEM((3 * comps, cells // LANES, own, LANES), F32),
            pltpu.VMEM((total, depth), BF16),
            pltpu.VMEM((total, depth), BF16),
            pltpu.VMEM((total, depth), BF16),
        ],
        input_output_aliases=aliases,
        compiler_params=pltpu.CompilerParams(vmem_limit_bytes=vmem_mib * 2**20),
        name="plane_terms",
    )(*operands)


def scatter_sum(held, order):
    count = lax.axis_size("grid")
    bits = count.bit_length() - 1
    me = lax.axis_index("grid")
    left = list(range(bits - 1, 0, -1))
    for bit in order:
        axis = left.index(bit)
        left.pop(axis)
        mine = (me >> bit) & 1
        send = lax.dynamic_index_in_dim(held, 1 - mine, axis, keepdims=False).astype(BF16)
        keep = lax.dynamic_index_in_dim(held, mine, axis, keepdims=False)
        held = keep + lax.ppermute(send, "grid", [(i, i ^ (1 << bit)) for i in range(count)]).astype(F32)
    return held


def gather_planes(own, blocks):
    arrived = []
    for plane in own:
        parts = [plane]
        for s in range(1, blocks):
            straight = s == blocks - 1
            source = plane if straight else parts[-1]
            parts.append(lax.ppermute(source, "mode", shift(blocks, -1 if straight else 1)))
        arrived.append(parts)
    return arrived


def per_device(held_modes, new_modes):
    held_own, new_own = held_modes.shape[0], new_modes.shape[0]
    comps, planes = held_modes.shape[1:3]
    cells = held_modes.shape[3] * held_modes.shape[4]
    count, blocks = lax.axis_size("grid"), lax.axis_size("mode")
    bits = count.bit_length() - 1
    weighting = 1.0 / math.sqrt(planes * cells * count)
    own = jnp.concatenate([held_modes, new_modes], 0)
    own = own.transpose(2, 1, 0, 3, 4).reshape(planes, comps, held_own + new_own, cells)
    own = [own[x] for x in range(planes)]
    place = jnp.stack([lax.axis_index("mode"), lax.axis_index("grid") & 1]).astype(jnp.int32)
    padded = [
        lax.ppermute(own[-1], "grid", shift(count, 1)),
        *own,
        lax.ppermute(own[0], "grid", shift(count, -1)),
    ]
    arrived = gather_planes(own, blocks)
    totals = None
    for x in range(planes):
        last = x == planes - 1
        around = padded[x : x + 3]
        ends = plane_terms(place, *around, arrived[x], totals, last, held_own, new_own, count)
        totals = ends[0]
    keep, send = ends
    sums = keep + lax.ppermute(send, "grid", [(i, i ^ 1) for i in range(count)]).astype(F32)
    sums = sums.reshape((2,) * (bits - 1) + (-1, sums.shape[1]))
    middle = sums.shape[-1] // 2 // LANES * LANES
    left = scatter_sum(sums[..., :middle], list(range(1, bits))) * weighting
    right = scatter_sum(sums[..., middle:], list(range(bits - 1, 0, -1))) * weighting
    new_third = new_own * (held_own + new_own) * blocks
    held_third = held_own * new_own * blocks
    rest = new_third + held_third - middle
    return (
        left[:, :new_third],
        jnp.concatenate([left[:, new_third:], right[:, :rest]], 1),
        right[: held_own * blocks // count, rest:],
    )


def solution(mesh):
    placed = (P("mode", None, "grid", None, None), P("mode", None, "grid", None, None))

    def step(held_modes, new_modes):
        body = jax.shard_map(
            per_device,
            mesh=mesh,
            in_specs=placed,
            out_specs=(P("grid", "mode"), P("grid", "mode"), P("grid", "mode")),
            check_vma=False,
        )
        return body(held_modes, new_modes)

    return step
```
